128 devices in a mesh: row: 16 (over y, x), col: 8 (over z, core).
Axes of the slice: x: 4, y: 4, z: 4, core: 2. Of those that a mesh axis runs over, the one named last changes fastest.
Arguments:
- amplitudes: bfloat16 [16384, 3072], P(('row', 'col')), may hold values from -6 to 6
- integrals: bfloat16 [8, 3072, 9600], P('col', None, 'row'), may hold values from -0.109375 to 0.109375
- irreps: int32 [16384], P(('row', 'col')), may hold values from 0 to 7, as said below
- row_mirror: int32 [16384], P(('row', 'col')), may hold values from 0 to 127, as said below
- col_mirror: int32 [9600], replicated, may hold values from 0 to 9599, as said below
Outputs:
- symmetrized: bfloat16 [16384, 9600], P(('row', 'col'))
The draws below stay inside these ranges and needn't reach their ends.
Inputs may be any that keep to these rules, and one draw needn't show every extreme that they name: `irreps`: among the 128 pairs of one block, no irrep occurs more than 32 times; in every block one irrep, the same for all blocks, occurs exactly 32 times. A pair and its mirrored partner have the same irrep. `row_mirror`: within each block of 128 pairs the map is an involution without fixed points. `col_mirror`: an involution of the 9600 slab columns without fixed points.
All inputs are finite; a program needn't handle non-finite values.
Results may differ from the reference program's by a relative error of at most 0.0051.
Values may be sent and summed in bfloat16 or wider, within the bound.
A program may use at most 192 MiB of HBM per device.

```python
import jax
import jax.numpy as jnp
from jax import lax

IRREPS = 8
KW = 3072
ROWS_DEV = 128
CAP = 32
SLAB = 9600
PAIRS = 16384


def ticket_layout(key):
    blocks = PAIRS // ROWS_DEV
    pair_count = ROWS_DEV // 2
    half_cap = CAP // 2
    base_key = jax.random.fold_in(key, 11)
    compelled_pick = jax.random.randint(jax.random.fold_in(base_key, 1), (), 0, IRREPS)
    priority_order = jax.random.permutation(jax.random.fold_in(base_key, 2), IRREPS).astype(jnp.int32)
    voucher_list = jnp.repeat(jnp.arange(IRREPS, dtype=jnp.int32), half_cap)
    voucher_count = IRREPS * half_cap

    def one_block(block_key):
        random_jitter = jax.random.randint(jax.random.fold_in(block_key, 3), (voucher_count,), 0, 65536)
        extra_reward = priority_order[voucher_list] * 16384 + jnp.where(voucher_list == compelled_pick, 262144, 0)
        merit_value = (random_jitter + extra_reward) * voucher_count + jnp.arange(voucher_count, dtype=jnp.int32)
        order = jnp.argsort(-merit_value, stable=True)
        chosen = voucher_list[order[:pair_count]]
        places = jax.random.permutation(jax.random.fold_in(block_key, 4), ROWS_DEV).astype(jnp.int32)
        first = places[0::2]
        second = places[1::2]
        labels = jnp.zeros((ROWS_DEV,), jnp.int32).at[first].set(chosen).at[second].set(chosen)
        partner = jnp.zeros((ROWS_DEV,), jnp.int32).at[first].set(second).at[second].set(first)
        return (labels, partner)
    block_keys = jax.random.split(base_key, blocks)
    labels, partner = jax.vmap(one_block)(block_keys)
    return (labels.reshape(-1), partner.reshape(-1))


def draw_irreps(key, part):
    return ticket_layout(key)[0]


def draw_row_mirror(key, part):
    return ticket_layout(key)[1]


def draw_col_mirror(key, part):
    places = jax.random.permutation(jax.random.fold_in(key, 29), SLAB).astype(jnp.int32)
    first = places[0::2]
    second = places[1::2]
    return jnp.zeros((SLAB,), jnp.int32).at[first].set(second).at[second].set(first)


def shard_levels(own_key, shape, cuts, low, high):
    level, own = 1.0, jax.random.fold_in(own_key, 6)
    for axis_at, parts in cuts:
        draws = jnp.exp(jax.random.uniform(jax.random.fold_in(own, axis_at), (parts,), jnp.float32, low / len(cuts), high / len(cuts)))
        level = level * jnp.repeat(draws, shape[axis_at] // parts).reshape([-1 if axis == axis_at else 1 for axis in range(len(shape))])
    return level


def scatter_about(rng, shape, deviation, limit, shards=(), kind=jnp.bfloat16):
    drawn = jax.random.normal(rng, shape, jnp.float32) * deviation
    if len(shards) > 0:
        drawn = shard_levels(rng, shape, shards, -0.22, 0.18) * drawn
    return jnp.clip(drawn, min=-limit, max=limit).astype(kind)


def setup_inputs(seed: int = 0) -> dict:
    key_of = jax.random.split(jax.random.key(seed), 6)
    return {
        "amplitudes": scatter_about(key_of[0], (PAIRS, KW), 1.0, 6.0, ((0, 128),)),
        "integrals": scatter_about(key_of[1], (IRREPS, KW, SLAB), KW ** -0.5, 0.109375, ((0, 8), (2, 16))),
        "irreps": draw_irreps(jax.random.fold_in(key_of[5], 71), 0),
        "row_mirror": draw_row_mirror(jax.random.fold_in(key_of[5], 71), 0),
        "col_mirror": draw_col_mirror(jax.random.fold_in(key_of[5], 71), 0),
    }


def multiply_irrep(operands):
    slot_rows, weight = operands
    return jnp.dot(slot_rows, weight, preferred_element_type=jnp.float32).astype(jnp.bfloat16)


def reference(amplitudes, integrals, irreps, row_mirror, col_mirror):
    blocks = PAIRS // ROWS_DEV
    irrep_grid = irreps.reshape(blocks, ROWS_DEV).astype(jnp.int32)
    onehot = (irrep_grid[:, :, None] == jnp.arange(IRREPS, dtype=jnp.int32)[None, None, :]).astype(jnp.int32)
    before = jnp.cumsum(onehot, axis=1) - onehot
    slot_index = jnp.sum(before * onehot, axis=2).astype(jnp.int32)
    block_ids = jnp.arange(blocks, dtype=jnp.int32)[:, None]
    position = (irrep_grid * (blocks * CAP) + block_ids * CAP + slot_index).reshape(-1).astype(jnp.int32)
    buffer = jnp.zeros((IRREPS * blocks * CAP, KW), jnp.bfloat16).at[position].set(amplitudes)
    buffer = buffer.reshape(IRREPS, blocks * CAP, KW)
    ladder_slots = lax.map(multiply_irrep, (buffer, integrals))
    ladder = ladder_slots.reshape(IRREPS * blocks * CAP, SLAB)[position]
    partner = ((jnp.arange(PAIRS, dtype=jnp.int32) // ROWS_DEV) * ROWS_DEV + row_mirror.astype(jnp.int32)).astype(jnp.int32)
    mirrored = ladder[partner][:, col_mirror.astype(jnp.int32)]
    return (ladder.astype(jnp.float32) + mirrored.astype(jnp.float32)).astype(jnp.bfloat16)
```

```python
import functools

import jax
import jax.numpy as jnp
from jax import lax
from jax.experimental import pallas as pl
from jax.experimental.pallas import tpu as pltpu
from jax.sharding import PartitionSpec as P

IRREPS = 8
KW = 3072
HALF = KW // 2
ROWS = 128
CAP = 32
SLOTS = IRREPS * CAP
COLS = 600
SLAB = 9600
NB = 16
NC = 5
CH = COLS // NC
MESH = pl.DeviceIdType.MESH
BF = jnp.bfloat16
F32 = jnp.float32


def ladder_kernel(
    amp_ref, w_ref, irr_ref,
    t_ref, a_all, w_all,
    xbuf, wbuf, abuf, pbuf, ys, tbuf, pos,
    ws, wr, rs, rr, ps, pr, ts, tr, ls, al, wl,
):
    row = lax.axis_index("row")
    col = lax.axis_index("col")
    y = row // 4
    x = row % 4
    z = col // 2
    core = col % 2

    def plane(dx, dy):
        return {"row": ((y + dy) % 4) * 4 + (x + dx) % 4, "col": col}

    def line(dz):
        return {"row": row, "col": ((z + dz) % 4) * 2 + core}

    sibling = {"row": row, "col": z * 2 + (1 - core)}

    def remote(src, dst, send, recv, where):
        return pltpu.make_async_remote_copy(
            src_ref=src, dst_ref=dst, send_sem=send, recv_sem=recv, device_id=where, device_id_type=MESH
        )

    def zop(j, name):
        rows = pl.ds(pl.multiple_of(j * CH, 8), CH)
        if name == "plus":
            return remote(w_ref.at[rows], w_all.at[4, rows], ws.at[j, 4], wr.at[j, 4], line(1))
        if name == "minus":
            return remote(w_ref.at[rows], w_all.at[2, rows], ws.at[j, 2], wr.at[j, 2], line(3))
        if name == "far0":
            k = pl.ds(0, HALF)
            return remote(w_all.at[4, rows, k], w_all.at[6, rows, k], ws.at[j, 6], wr.at[j, 6], line(1))
        if name == "far1":
            k = pl.ds(HALF, HALF)
            return remote(w_all.at[2, rows, k], w_all.at[6, rows, k], ws.at[j, 0], wr.at[j, 0], line(3))
        slot = {"sib2": 2, "sib4": 4, "sib6": 6}[name]
        return remote(
            w_all.at[slot, rows], w_all.at[slot + 1, rows], ws.at[j, slot + 1], wr.at[j, slot + 1], sibling
        )

    def sibown():
        return remote(w_ref, w_all.at[1], ws.at[0, 1], wr.at[0, 1], sibling)

    def slot(h, d1, d2):
        return d2 * 4 + d1 if h == 0 else d1 * 4 + d2

    def rop(h, phase, n):
        d1 = 0 if phase == 4 else phase
        if phase == 4:
            place = lambda d: slot(h, d, 0)
            to = lambda s: plane(s, 0) if h == 0 else plane(0, s)
        else:
            place = lambda d: slot(h, d1, d)
            to = lambda s: plane(0, s) if h == 0 else plane(s, 0)
        full, first, second = pl.ds(64 * h, 64), pl.ds(64 * h, 32), pl.ds(64 * h + 32, 32)
        source, target, part, way = (
            (0, 3, full, 1), (0, 1, full, 3), (3, 2, first, 1), (1, 2, second, 3)
        )[n]
        k = place(source)
        src = amp_ref.at[part] if k == 0 else a_all.at[k, part]
        return remote(
            src, a_all.at[place(target), part], rs.at[h, phase, n], rr.at[h, phase, n], to(way)
        )

    def pop(k):
        dx, dy = k % 4, k // 4
        there = ((4 - dy) % 4) * 4 + (4 - dx) % 4
        return remote(pos.at[0], pos.at[there], ps.at[there], pr.at[there], plane(dx, dy))

    def top(j, k):
        rows = pl.ds(pl.multiple_of(row * COLS + j * CH, 8), CH)
        return remote(tbuf.at[j, k], t_ref.at[rows], ts.at[j], tr.at[j], plane(k % 4, k // 4))

    barrier = pltpu.get_barrier_semaphore()

    def greet(k, c):
        pl.semaphore_signal(barrier, inc=1, device_id=plane(k % 4, k // 4), device_id_type=MESH)
        return c

    lax.fori_loop(1, NB, greet, 0)
    for where in (line(1), line(3), sibling):
        pl.semaphore_signal(barrier, inc=1, device_id=where, device_id_type=MESH)
    pl.semaphore_wait(barrier, NB + 2)

    for j in range(2):
        zop(j, "plus").start()
        zop(j, "minus").start()
    for phase in (4, 0):
        for h in range(2):
            rop(h, phase, 0).start()
            rop(h, phase, 1).start()
    sibown().start()
    own_w = pltpu.make_async_copy(w_ref, w_all.at[0], ls.at[NC])
    own_w.start()
    own_a = pltpu.make_async_copy(amp_ref, a_all.at[0], ls.at[NC + 1])
    own_a.start()

    irr = irr_ref[...]
    onehot = (lax.broadcasted_iota(jnp.int32, (IRREPS, ROWS), 0) == irr).astype(F32)
    earlier = (
        lax.broadcasted_iota(jnp.int32, (ROWS, ROWS), 0) < lax.broadcasted_iota(jnp.int32, (ROWS, ROWS), 1)
    ).astype(F32)
    before = jnp.dot(onehot.astype(BF), earlier.astype(BF), preferred_element_type=F32)
    rank = jnp.sum(before * onehot, axis=0, keepdims=True)
    place = irr.astype(F32) * CAP + rank
    pos[0] = jnp.broadcast_to(place, (8, ROWS))

    def send_pos(k, c):
        pop(k).start()
        return c

    lax.fori_loop(1, NB, send_pos, 0)

    def pass_on(j):
        zop(j, "plus").wait_recv()
        zop(j, "far0").start()
        zop(j, "sib4").start()
        zop(j, "minus").wait_recv()
        zop(j, "far1").start()
        zop(j, "sib2").start()

    def own_chunk(j):
        zop(j, "plus").start()
        zop(j, "minus").start()

    def ring_pass(phase):
        for h in range(2):
            rop(h, phase, 0).wait_recv()
            rop(h, phase, 2).start()
            rop(h, phase, 1).wait_recv()
            rop(h, phase, 3).start()

    def ring_send(phase):
        for h in range(2):
            rop(h, phase, 0).start()
            rop(h, phase, 1).start()

    ring_pass(4)
    ring_send(3)
    ring_send(1)
    for h in range(2):
        rop(h, 4, 2).wait_recv()
        rop(h, 4, 3).wait_recv()
    ring_send(2)
    ring_pass(0)
    pass_on(0)
    own_chunk(2)
    ring_pass(3)
    ring_pass(1)
    pass_on(1)
    own_chunk(3)
    ring_pass(2)
    for phase in (0, 3, 1, 2):
        for h in range(2):
            rop(h, phase, 2).wait_recv()
            rop(h, phase, 3).wait_recv()
    own_a.wait()
    own_w.wait()

    def wait_pos(k, c):
        pop(k).wait_recv()
        return c

    lax.fori_loop(1, NB, wait_pos, 0)

    def aload(k, buf):
        return pltpu.make_async_copy(a_all.at[k], abuf.at[buf], al.at[buf])

    aload(0, 0).start()

    def sort_block(k, c):
        buf = k % 2

        @pl.when(k + 1 < NB)
        def _():
            aload(k + 1, 1 - buf).start()

        hot = (
            lax.broadcasted_iota(jnp.int32, (SLOTS, ROWS), 0).astype(F32) == pos[k][0:1, :]
        ).astype(F32).astype(BF)
        pbuf[k] = hot
        aload(k, buf).wait()
        for n in range(6):
            lanes = pl.ds(n * 512, 512)
            got = jnp.dot(hot, abuf[buf, :, lanes], preferred_element_type=F32).astype(BF)
            xbuf[:, pl.ds(pl.multiple_of(k * CAP, CAP), CAP), lanes] = got.reshape(IRREPS, CAP, 512)
        return c

    lax.fori_loop(0, NB, sort_block, 0)

    def wload(j, n):
        rows = pl.ds(pl.multiple_of(j * CH, 8), CH)
        return pltpu.make_async_copy(w_all.at[n, rows], wbuf.at[n], wl.at[n])

    def chunk(j, c):
        @pl.when(j + 2 < NC)
        def _():
            pass_on(j + 2)

        @pl.when(j + 4 < NC)
        def _():
            own_chunk(j + 4)

        @pl.when(j == 0)
        def _():
            sibown().wait_recv()

        zop(j, "sib2").wait_recv()
        zop(j, "sib4").wait_recv()
        for n in range(6):
            wload(j, n).start()

        def irrep(n, c):
            @pl.when(n == 5)
            def _():
                zop(j, "far0").wait_recv()
                zop(j, "far1").wait_recv()
                zop(j, "sib6").start()
                wload(j, 6).start()

            @pl.when(n == 7)
            def _():
                zop(j, "sib6").wait_recv()
                wload(j, 7).start()

            m = n // 2
            dz = m + m // 2 - 2 * (m // 3)
            which = 2 * ((z + dz) % 4) + (core + n % 2) % 2
            wload(j, n).wait()
            got = lax.dot_general(
                xbuf[which], wbuf[n], (((1,), (1,)), ((), ())), preferred_element_type=F32
            ).astype(BF)
            ys[:, pl.ds(pl.multiple_of(which * CAP, CAP), CAP), 0:CH] = got.reshape(NB, CAP, CH)
            return c

        lax.fori_loop(0, IRREPS, irrep, 0)

        def back(k, c):
            tbuf[j, k] = lax.dot_general(
                ys[k], pbuf[k], (((0,), (0,)), ((), ())), preferred_element_type=F32
            )[0:CH].astype(BF)

            @pl.when(k > 0)
            def _():
                top(j, k).start()

            return c

        lax.fori_loop(0, NB, back, 0)
        rows = pl.ds(pl.multiple_of(row * COLS + j * CH, 8), CH)
        pltpu.make_async_copy(tbuf.at[j, 0], t_ref.at[rows], ls.at[j]).start()
        return c

    lax.fori_loop(0, NC, chunk, 0)

    def finish(j, c):
        rows = pl.ds(pl.multiple_of(row * COLS + j * CH, 8), CH)
        pltpu.make_async_copy(tbuf.at[j, 0], t_ref.at[rows], ls.at[j]).wait()
        some = t_ref.at[pl.ds(0, (NB - 1) * CH)]
        pltpu.make_async_copy(some, some, ts.at[j]).wait()
        pltpu.make_async_copy(some, some, tr.at[j]).wait()
        for name in ("plus", "minus", "far0", "far1", "sib2", "sib4", "sib6"):
            zop(j, name).wait_send()
        return c

    lax.fori_loop(0, NC, finish, 0)
    sibown().wait_send()
    for phase in range(5):
        for h in range(2):
            for n in range(4):
                rop(h, phase, n).wait_send()

    def done_pos(k, c):
        pop(k).wait_send()
        return c

    lax.fori_loop(1, NB, done_pos, 0)


def ladder(amplitudes, integrals, irreps):
    dma = pltpu.SemaphoreType.DMA
    hbm = pl.BlockSpec(memory_space=pl.ANY)
    t, _, _ = pl.pallas_call(
        ladder_kernel,
        out_shape=(
            jax.ShapeDtypeStruct((SLAB, ROWS), BF),
            jax.ShapeDtypeStruct((NB, ROWS, KW), BF),
            jax.ShapeDtypeStruct((IRREPS, COLS, KW), BF),
        ),
        in_specs=[hbm, hbm, pl.BlockSpec(memory_space=pltpu.VMEM)],
        out_specs=(hbm, hbm, hbm),
        scratch_shapes=[
            pltpu.VMEM((IRREPS, NB * CAP, KW), BF),
            pltpu.VMEM((IRREPS, CH, KW), BF),
            pltpu.VMEM((2, ROWS, KW), BF),
            pltpu.VMEM((NB, SLOTS, ROWS), BF),
            pltpu.VMEM((NB, SLOTS, 128), BF),
            pltpu.VMEM((NC, NB, CH, ROWS), BF),
            pltpu.VMEM((NB, 8, ROWS), F32),
            dma((NC, 8)),
            dma((NC, 8)),
            dma((2, 5, 4)),
            dma((2, 5, 4)),
            dma((NB,)),
            dma((NB,)),
            dma((NC,)),
            dma((NC,)),
            dma((NC + 2,)),
            dma((2,)),
            dma((8,)),
        ],
        compiler_params=pltpu.CompilerParams(
            collective_id=0, has_side_effects=True, vmem_limit_bytes=56 * 1024 * 1024
        ),
        name="ladder",
    )(amplitudes, integrals, irreps)
    return t


GB = 384
NG = SLAB // GB
UNROLL = 16


def mirror_kernel(col_ref, t_ref, row_ref, out_ref, tf, g):
    def widen(i, c):
        rows = pl.ds(pl.multiple_of(i * GB, GB), GB)
        tf[rows, :] = t_ref[rows, :].astype(F32)
        return c

    lax.fori_loop(0, NG, widen, 0)
    lane = lax.broadcasted_iota(jnp.int32, (ROWS, ROWS), 1)
    sub = lax.broadcasted_iota(jnp.int32, (ROWS, ROWS), 0)
    same = (lane == sub).astype(F32).astype(BF)
    swap = (sub == row_ref[...]).astype(F32).astype(BF)

    def block(i, c):
        base = pl.multiple_of(i * GB, GB)

        def pick(u, c):
            for r in range(UNROLL):
                at = u * UNROLL + r
                g[pl.ds(at, 1), :] = tf[pl.ds(col_ref[base + at], 1), :]
            return c

        lax.fori_loop(0, GB // UNROLL, pick, 0)
        nt = (((1,), (1,)), ((), ()))
        here = lax.dot_general(same, t_ref[pl.ds(base, GB), :], nt, preferred_element_type=F32)
        there = lax.dot_general(swap, g[...].astype(BF), nt, preferred_element_type=F32)
        out_ref[:, pl.ds(base, GB)] = (here + there).astype(BF)
        return c

    lax.fori_loop(0, NG, block, 0)


def mirror(t, row_mirror, col_mirror):
    vmem = pl.BlockSpec(memory_space=pltpu.VMEM)
    return pl.pallas_call(
        mirror_kernel,
        out_shape=jax.ShapeDtypeStruct((ROWS, SLAB), BF),
        in_specs=[pl.BlockSpec(memory_space=pltpu.SMEM), vmem, vmem],
        out_specs=vmem,
        scratch_shapes=[pltpu.VMEM((SLAB, ROWS), F32), pltpu.VMEM((GB, ROWS), F32)],
        compiler_params=pltpu.CompilerParams(vmem_limit_bytes=32 * 1024 * 1024),
        name="mirror",
    )(col_mirror, t, row_mirror)


def body(amplitudes, integrals, irreps, row_mirror, col_mirror):
    w = jnp.swapaxes(integrals[0], 0, 1)
    t = ladder(amplitudes, w, irreps.reshape(1, ROWS))
    return mirror(t, row_mirror.reshape(1, ROWS), col_mirror)


def solution(mesh):
    return jax.shard_map(
        body,
        mesh=mesh,
        in_specs=(
            P(("row", "col"), None),
            P("col", None, "row"),
            P(("row", "col")),
            P(("row", "col")),
            P(),
        ),
        out_specs=P(("row", "col"), None),
        check_vma=False,
    )
```

```python
import functools

import jax
import jax.numpy as jnp
from jax import lax
from jax.experimental import pallas as pl
from jax.experimental.pallas import tpu as pltpu
from jax.sharding import PartitionSpec as P

IRREPS = 8
KW = 3072
HALF = KW // 2
ROWS = 128
CAP = 32
SLOTS = IRREPS * CAP
COLS = 600
SLAB = 9600
NB = 16
PIECES = (128, 128, 128, 128, 48, 40)
STARTS = (0, 128, 256, 384, 512, 560)
NP = len(PIECES)
CHUNKS = ((0, 1), (2, 3), (4, 5))
NC = len(CHUNKS)
WIDE = 256
NARROW = 88
ABUFS = 4
MESH = pl.DeviceIdType.MESH
BF = jnp.bfloat16
F32 = jnp.float32


def ladder_kernel(
    amp_ref, w_ref, irr_ref,
    t_ref, a_all, w_all,
    xbuf, wbuf, wlast, abuf, pbuf, ys, ylast, tbuf, tlast, pos,
    ws, wr, rs, rr, ps, pr, ts, tr, ls, al, wl,
):
    row = lax.axis_index("row")
    col = lax.axis_index("col")
    y = row // 4
    x = row % 4
    z = col // 2
    core = col % 2

    def plane(dx, dy):
        return {"row": ((y + dy) % 4) * 4 + (x + dx) % 4, "col": col}

    def line(dz):
        return {"row": row, "col": ((z + dz) % 4) * 2 + core}

    sibling = {"row": row, "col": z * 2 + (1 - core)}

    def remote(src, dst, send, recv, where):
        return pltpu.make_async_remote_copy(
            src_ref=src, dst_ref=dst, send_sem=send, recv_sem=recv, device_id=where, device_id_type=MESH
        )

    def zop(j, name):
        rows = pl.ds(STARTS[j], PIECES[j])
        if name == "plus":
            return remote(w_ref.at[rows], w_all.at[4, rows], ws.at[j, 4], wr.at[j, 4], line(1))
        if name == "minus":
            return remote(w_ref.at[rows], w_all.at[2, rows], ws.at[j, 2], wr.at[j, 2], line(3))
        if name == "far0":
            k = pl.ds(0, HALF)
            return remote(w_all.at[4, rows, k], w_all.at[6, rows, k], ws.at[j, 6], wr.at[j, 6], line(1))
        if name == "far1":
            k = pl.ds(HALF, HALF)
            return remote(w_all.at[2, rows, k], w_all.at[6, rows, k], ws.at[j, 0], wr.at[j, 0], line(3))
        slot = {"sib2": 2, "sib4": 4, "sib6": 6}[name]
        return remote(
            w_all.at[slot, rows], w_all.at[slot + 1, rows], ws.at[j, slot + 1], wr.at[j, slot + 1], sibling
        )

    def sibown():
        return remote(w_ref, w_all.at[1], ws.at[0, 1], wr.at[0, 1], sibling)

    def slot(h, d1, d2):
        return d2 * 4 + d1 if h == 0 else d1 * 4 + d2

    def rop(h, phase, n):
        d1 = 0 if phase == 4 else phase
        if phase == 4:
            place = lambda d: slot(h, d, 0)
            to = lambda s: plane(s, 0) if h == 0 else plane(0, s)
        else:
            place = lambda d: slot(h, d1, d)
            to = lambda s: plane(0, s) if h == 0 else plane(s, 0)
        full, first, second = pl.ds(64 * h, 64), pl.ds(64 * h, 32), pl.ds(64 * h + 32, 32)
        source, target, part, way = (
            (0, 3, full, 1), (0, 1, full, 3), (3, 2, first, 1), (1, 2, second, 3)
        )[n]
        k = place(source)
        src = amp_ref.at[part] if k == 0 else a_all.at[k, part]
        return remote(
            src, a_all.at[place(target), part], rs.at[h, phase, n], rr.at[h, phase, n], to(way)
        )

    def pop(k):
        dx, dy = k % 4, k // 4
        there = ((4 - dy) % 4) * 4 + (4 - dx) % 4
        return remote(pos.at[0], pos.at[there], ps.at[there], pr.at[there], plane(dx, dy))

    def width(c):
        return sum(PIECES[j] for j in CHUNKS[c])

    def out_rows(c):
        return pl.ds(pl.multiple_of(row * COLS + STARTS[CHUNKS[c][0]], 8), width(c))

    def staged(c, k):
        return tbuf.at[c, k, pl.ds(0, width(c))] if c < NC - 1 else tlast.at[k]

    def top(c, k):
        return remote(staged(c, k), t_ref.at[out_rows(c)], ts.at[c], tr.at[c], plane(k % 4, k // 4))

    def keep(c):
        return pltpu.make_async_copy(staged(c, 0), t_ref.at[out_rows(c)], ls.at[c])

    barrier = pltpu.get_barrier_semaphore()

    def greet(k, c):
        pl.semaphore_signal(barrier, inc=1, device_id=plane(k % 4, k // 4), device_id_type=MESH)
        return c

    lax.fori_loop(1, NB, greet, 0)
    for where in (line(1), line(3), sibling):
        pl.semaphore_signal(barrier, inc=1, device_id=where, device_id_type=MESH)
    pl.semaphore_wait(barrier, NB + 2)

    for j in range(2):
        zop(j, "plus").start()
        zop(j, "minus").start()
    for phase in (4, 0):
        for h in range(2):
            rop(h, phase, 0).start()
            rop(h, phase, 1).start()
    sibown().start()

    irr = irr_ref[...]
    onehot = (lax.broadcasted_iota(jnp.int32, (IRREPS, ROWS), 0) == irr).astype(F32)
    earlier = (
        lax.broadcasted_iota(jnp.int32, (ROWS, ROWS), 0) < lax.broadcasted_iota(jnp.int32, (ROWS, ROWS), 1)
    ).astype(F32)
    before = jnp.dot(onehot.astype(BF), earlier.astype(BF), preferred_element_type=F32)
    rank = jnp.sum(before * onehot, axis=0, keepdims=True)
    place = irr.astype(F32) * CAP + rank
    pos[0] = jnp.broadcast_to(place, (8, ROWS))

    def send_pos(k, c):
        pop(k).start()
        return c

    lax.fori_loop(1, NB, send_pos, 0)

    def pass_on(j):
        zop(j, "plus").wait_recv()
        zop(j, "far0").start()
        zop(j, "sib4").start()
        zop(j, "minus").wait_recv()
        zop(j, "far1").start()
        zop(j, "sib2").start()

    def own_chunk(j):
        zop(j, "plus").start()
        zop(j, "minus").start()

    def ring_pass(phase):
        for h in range(2):
            rop(h, phase, 0).wait_recv()
            rop(h, phase, 2).start()
            rop(h, phase, 1).wait_recv()
            rop(h, phase, 3).start()

    def ring_send(phase):
        for h in range(2):
            rop(h, phase, 0).start()
            rop(h, phase, 1).start()

    ring_pass(4)
    ring_send(3)
    ring_send(1)
    for h in range(2):
        rop(h, 4, 2).wait_recv()
        rop(h, 4, 3).wait_recv()
    ring_send(2)
    ring_pass(0)
    pass_on(0)
    own_chunk(2)
    ring_pass(3)
    ring_pass(1)
    pass_on(1)
    own_chunk(3)
    ring_pass(2)
    pass_on(2)
    for phase in (0, 3, 1, 2):
        for h in range(2):
            rop(h, phase, 2).wait_recv()
            rop(h, phase, 3).wait_recv()

    def wait_pos(k, c):
        pop(k).wait_recv()
        return c

    lax.fori_loop(1, NB, wait_pos, 0)

    def wload(j, n):
        if j < CHUNKS[-1][0]:
            there = wbuf.at[n, pl.ds(128 * (j % 2), PIECES[j])]
        else:
            there = wlast.at[n, pl.ds(STARTS[j] - STARTS[CHUNKS[-1][0]], PIECES[j])]
        src = w_ref if n == 0 else w_all.at[n]
        return pltpu.make_async_copy(src.at[pl.ds(STARTS[j], PIECES[j])], there, wl.at[j, n])

    def near(c):
        for j in CHUNKS[c]:
            if j == 0:
                sibown().wait_recv()
            zop(j, "sib2").wait_recv()
            zop(j, "sib4").wait_recv()
            for n in range(6):
                wload(j, n).start()

    def far(c):
        for j in CHUNKS[c]:
            zop(j, "far0").wait_recv()
            zop(j, "far1").wait_recv()
            zop(j, "sib6").start()
            wload(j, 6).start()
        for j in CHUNKS[c]:
            zop(j, "sib6").wait_recv()
            wload(j, 7).start()

    def aload(k):
        return pltpu.make_async_copy(a_all.at[k], abuf.at[k % ABUFS], al.at[k % ABUFS])

    def sort_block(k, c):
        hot = (
            lax.broadcasted_iota(jnp.int32, (SLOTS, ROWS), 0).astype(F32) == pos[k][0:1, :]
        ).astype(F32).astype(BF)
        pbuf[k] = hot
        aload(k).wait()
        for n in range(6):
            lanes = pl.ds(n * 512, 512)
            got = jnp.dot(hot, abuf[k % ABUFS, :, lanes], preferred_element_type=F32).astype(BF)
            xbuf[:, pl.ds(pl.multiple_of(k * CAP, CAP), CAP), lanes] = got.reshape(IRREPS, CAP, 512)

        @pl.when(k + ABUFS < NB)
        def _():
            aload(k + ABUFS).start()

        return c

    def multiply(c, first, last):
        last_chunk = c == NC - 1

        def irrep(n, carry):
            m = n // 2
            dz = m + m // 2 - 2 * (m // 3)
            which = 2 * ((z + dz) % 4) + (core + n % 2) % 2
            got = lax.dot_general(
                xbuf[which],
                wlast[n] if last_chunk else wbuf[n],
                (((1,), (1,)), ((), ())),
                preferred_element_type=F32,
            ).astype(BF)
            at = pl.ds(pl.multiple_of(which * CAP, CAP), CAP)
            if last_chunk:
                ylast[:, at, 0:NARROW] = got.reshape(NB, CAP, NARROW)
            else:
                ys[:, at, :] = got.reshape(NB, CAP, WIDE)
            return carry

        for j in CHUNKS[c]:
            for n in range(first, last):
                wload(j, n).wait()
        lax.fori_loop(first, last, irrep, 0)

    def give_back(c):
        last_chunk = c == NC - 1

        def back(u, carry):
            for v in range(4):
                k = 4 * u + v
                got = lax.dot_general(
                    ylast[k] if last_chunk else ys[k],
                    pbuf[k],
                    (((0,), (0,)), ((), ())),
                    preferred_element_type=F32,
                ).astype(BF)
                if last_chunk:
                    tlast[k] = got[0:NARROW]
                else:
                    tbuf[c, k] = got
            for v in range(4):
                if v == 0:

                    @pl.when(u > 0)
                    def _():
                        top(c, 4 * u).start()

                else:
                    top(c, 4 * u + v).start()
            return carry

        lax.fori_loop(0, NB // 4, back, 0)
        keep(c).start()

    pltpu.make_async_copy(amp_ref, abuf.at[0], al.at[0]).start()
    for k in range(1, ABUFS):
        aload(k).start()
    near(0)
    lax.fori_loop(0, NB, sort_block, 0)
    pass_on(3)
    own_chunk(4)
    own_chunk(5)
    multiply(0, 0, 6)
    far(0)
    multiply(0, 6, 8)
    near(1)
    give_back(0)
    multiply(1, 0, 6)
    far(1)
    multiply(1, 6, 8)
    give_back(1)
    pass_on(4)
    pass_on(5)
    near(2)
    multiply(2, 0, 6)
    far(2)
    multiply(2, 6, 8)
    give_back(2)

    for c in range(NC):
        keep(c).wait()
        some = t_ref.at[pl.ds(0, (NB - 1) * width(c))]
        pltpu.make_async_copy(some, some, ts.at[c]).wait()
        pltpu.make_async_copy(some, some, tr.at[c]).wait()
    for j in range(NP):
        for name in ("plus", "minus", "far0", "far1", "sib2", "sib4", "sib6"):
            zop(j, name).wait_send()
    sibown().wait_send()
    for phase in range(5):
        for h in range(2):
            for n in range(4):
                rop(h, phase, n).wait_send()

    def done_pos(k, c):
        pop(k).wait_send()
        return c

    lax.fori_loop(1, NB, done_pos, 0)


def ladder(amplitudes, integrals, irreps):
    dma = pltpu.SemaphoreType.DMA
    hbm = pl.BlockSpec(memory_space=pl.ANY)
    t, _, _ = pl.pallas_call(
        ladder_kernel,
        out_shape=(
            jax.ShapeDtypeStruct((SLAB, ROWS), BF),
            jax.ShapeDtypeStruct((NB, ROWS, KW), BF),
            jax.ShapeDtypeStruct((IRREPS, COLS, KW), BF),
        ),
        in_specs=[hbm, hbm, pl.BlockSpec(memory_space=pltpu.VMEM)],
        out_specs=(hbm, hbm, hbm),
        scratch_shapes=[
            pltpu.VMEM((IRREPS, NB * CAP, KW), BF),
            pltpu.VMEM((IRREPS, WIDE, KW), BF),
            pltpu.VMEM((IRREPS, NARROW, KW), BF),
            pltpu.VMEM((ABUFS, ROWS, KW), BF),
            pltpu.VMEM((NB, SLOTS, ROWS), BF),
            pltpu.VMEM((NB, SLOTS, WIDE), BF),
            pltpu.VMEM((NB, SLOTS, 128), BF),
            pltpu.VMEM((NC - 1, NB, WIDE, ROWS), BF),
            pltpu.VMEM((NB, NARROW, ROWS), BF),
            pltpu.VMEM((NB, 8, ROWS), F32),
            dma((NP, 8)),
            dma((NP, 8)),
            dma((2, 5, 4)),
            dma((2, 5, 4)),
            dma((NB,)),
            dma((NB,)),
            dma((NC,)),
            dma((NC,)),
            dma((NC,)),
            dma((ABUFS,)),
            dma((NP, 8)),
        ],
        compiler_params=pltpu.CompilerParams(
            collective_id=0, has_side_effects=True, vmem_limit_bytes=60 * 1024 * 1024
        ),
        name="ladder",
    )(amplitudes, integrals, irreps)
    return t


GB = 384
NG = SLAB // GB
NT = (((1,), (1,)), ((), ()))


def mirror_kernel(col_ref, t_ref, row_ref, out_ref, tf, even, odd):
    def widen(i, c):
        rows = pl.ds(pl.multiple_of(i * GB, GB), GB)
        tf[rows, :] = t_ref[rows, :].astype(F32)
        return c

    lax.fori_loop(0, NG, widen, 0)
    lane = lax.broadcasted_iota(jnp.int32, (ROWS, ROWS), 1)
    sub = lax.broadcasted_iota(jnp.int32, (ROWS, ROWS), 0)
    same = (lane == sub).astype(F32).astype(BF)
    swap = (sub == row_ref[...]).astype(F32).astype(BF)

    def pick(base, g):
        for q in range(GB // 8):
            some = [tf[pl.ds(col_ref[base + 8 * q + r], 1), :] for r in range(8)]
            g[8 * q : 8 * q + 8, :] = jnp.concatenate(some, axis=0)

    def add(base, g):
        here = lax.dot_general(same, t_ref[pl.ds(base, GB), :], NT, preferred_element_type=F32)
        there = lax.dot_general(swap, g[...].astype(BF), NT, preferred_element_type=F32)
        out_ref[:, pl.ds(base, GB)] = (here + there).astype(BF)

    pick(0, even)

    def two(i, c):
        first = pl.multiple_of(2 * i * GB, GB)
        second = pl.multiple_of(first + GB, GB)
        third = pl.multiple_of(first + 2 * GB, GB)
        pick(second, odd)
        add(first, even)
        pick(third, even)
        add(second, odd)
        return c

    lax.fori_loop(0, NG // 2, two, 0)
    add((NG - 1) * GB, even)


def mirror(t, row_mirror, col_mirror):
    vmem = pl.BlockSpec(memory_space=pltpu.VMEM)
    return pl.pallas_call(
        mirror_kernel,
        out_shape=jax.ShapeDtypeStruct((ROWS, SLAB), BF),
        in_specs=[pl.BlockSpec(memory_space=pltpu.SMEM), vmem, vmem],
        out_specs=vmem,
        scratch_shapes=[
            pltpu.VMEM((SLAB, ROWS), F32),
            pltpu.VMEM((GB, ROWS), F32),
            pltpu.VMEM((GB, ROWS), F32),
        ],
        compiler_params=pltpu.CompilerParams(vmem_limit_bytes=32 * 1024 * 1024),
        name="mirror",
    )(col_mirror, t, row_mirror)


def body(amplitudes, integrals, irreps, row_mirror, col_mirror):
    w = jnp.swapaxes(integrals[0], 0, 1)
    t = ladder(amplitudes, w, irreps.reshape(1, ROWS))
    return mirror(t, row_mirror.reshape(1, ROWS), col_mirror)


def solution(mesh):
    return jax.shard_map(
        body,
        mesh=mesh,
        in_specs=(
            P(("row", "col"), None),
            P("col", None, "row"),
            P(("row", "col")),
            P(("row", "col")),
            P(),
        ),
        out_specs=P(("row", "col"), None),
        check_vma=False,
    )
```

```python
import functools

import jax
import jax.numpy as jnp
from jax import lax
from jax.experimental import pallas as pl
from jax.experimental.pallas import tpu as pltpu
from jax.sharding import PartitionSpec as P

IRREPS = 8
KW = 3072
HALF = KW // 2
ROWS = 128
CAP = 32
SLOTS = IRREPS * CAP
COLS = 600
SLAB = 9600
NB = 16
PIECES = (128, 128, 128, 128, 48, 40)
STARTS = (0, 128, 256, 384, 512, 560)
NP = len(PIECES)
CHUNKS = ((0, 1), (2, 3), (4, 5))
NC = len(CHUNKS)
WIDE = 256
NARROW = 88
ABUFS = 4
MESH = pl.DeviceIdType.MESH
BF = jnp.bfloat16
F32 = jnp.float32


def ladder_kernel(
    amp_ref, w_ref, irr_ref,
    t_ref, a_all, w_all,
    xbuf, wbuf, wlast, abuf, pbuf, ys, ylast, tbuf, tlast, pos,
    ws, wr, rs, rr, ps, pr, ts, tr, ls, al, wl,
):
    row = lax.axis_index("row")
    col = lax.axis_index("col")
    y = row // 4
    x = row % 4
    z = col // 2
    core = col % 2

    def plane(dx, dy):
        return {"row": ((y + dy) % 4) * 4 + (x + dx) % 4, "col": col}

    def line(dz):
        return {"row": row, "col": ((z + dz) % 4) * 2 + core}

    sibling = {"row": row, "col": z * 2 + (1 - core)}

    def remote(src, dst, send, recv, where):
        return pltpu.make_async_remote_copy(
            src_ref=src, dst_ref=dst, send_sem=send, recv_sem=recv, device_id=where, device_id_type=MESH
        )

    def held(j, n, k=None):
        if j >= CHUNKS[-1][0]:
            rows = pl.ds(STARTS[j] - STARTS[CHUNKS[-1][0]], PIECES[j])
            return wlast.at[n, rows] if k is None else wlast.at[n, rows, k]
        rows = pl.ds(STARTS[j], PIECES[j])
        return w_all.at[n, rows] if k is None else w_all.at[n, rows, k]

    def zop(j, name):
        own = w_ref.at[pl.ds(STARTS[j], PIECES[j])]
        if name == "plus":
            return remote(own, held(j, 4), ws.at[j, 4], wr.at[j, 4], line(1))
        if name == "minus":
            return remote(own, held(j, 2), ws.at[j, 2], wr.at[j, 2], line(3))
        if name == "far0":
            k = pl.ds(0, HALF)
            return remote(held(j, 4, k), held(j, 6, k), ws.at[j, 6], wr.at[j, 6], line(1))
        if name == "far1":
            k = pl.ds(HALF, HALF)
            return remote(held(j, 2, k), held(j, 6, k), ws.at[j, 0], wr.at[j, 0], line(3))
        if name == "sib0":
            return remote(own, held(j, 1), ws.at[j, 1], wr.at[j, 1], sibling)
        slot = {"sib2": 2, "sib4": 4, "sib6": 6}[name]
        return remote(
            held(j, slot), held(j, slot + 1), ws.at[j, slot + 1], wr.at[j, slot + 1], sibling
        )

    def slot(h, d1, d2):
        return d2 * 4 + d1 if h == 0 else d1 * 4 + d2

    def rop(h, phase, n):
        d1 = 0 if phase == 4 else phase
        if phase == 4:
            place = lambda d: slot(h, d, 0)
            to = lambda s: plane(s, 0) if h == 0 else plane(0, s)
        else:
            place = lambda d: slot(h, d1, d)
            to = lambda s: plane(0, s) if h == 0 else plane(s, 0)
        full, first, second = pl.ds(64 * h, 64), pl.ds(64 * h, 32), pl.ds(64 * h + 32, 32)
        source, target, part, way = (
            (0, 3, full, 1), (0, 1, full, 3), (3, 2, first, 1), (1, 2, second, 3)
        )[n]
        k = place(source)
        src = amp_ref.at[part] if k == 0 else a_all.at[k, part]
        return remote(
            src, a_all.at[place(target), part], rs.at[h, phase, n], rr.at[h, phase, n], to(way)
        )

    def pop(k):
        dx, dy = k % 4, k // 4
        there = ((4 - dy) % 4) * 4 + (4 - dx) % 4
        return remote(pos.at[0], pos.at[there], ps.at[there], pr.at[there], plane(dx, dy))

    def width(c):
        return sum(PIECES[j] for j in CHUNKS[c])

    def out_rows(c):
        return pl.ds(pl.multiple_of(row * COLS + STARTS[CHUNKS[c][0]], 8), width(c))

    def staged(c, k):
        return tbuf.at[c, k, pl.ds(0, width(c))] if c < NC - 1 else tlast.at[k]

    def top(c, k):
        return remote(staged(c, k), t_ref.at[out_rows(c)], ts.at[c], tr.at[c], plane(k % 4, k // 4))

    def keep(c):
        return pltpu.make_async_copy(staged(c, 0), t_ref.at[out_rows(c)], ls.at[c])

    barrier = pltpu.get_barrier_semaphore()

    def greet(k, c):
        pl.semaphore_signal(barrier, inc=1, device_id=plane(k % 4, k // 4), device_id_type=MESH)
        return c

    lax.fori_loop(1, NB, greet, 0)
    for where in (line(1), line(3), sibling):
        pl.semaphore_signal(barrier, inc=1, device_id=where, device_id_type=MESH)
    pl.semaphore_wait(barrier, NB + 2)

    for j in range(2):
        zop(j, "plus").start()
        zop(j, "minus").start()
    for phase in (4, 0):
        for h in range(2):
            rop(h, phase, 0).start()
            rop(h, phase, 1).start()
    for j in range(NP):
        zop(j, "sib0").start()

    irr = irr_ref[...]
    onehot = (lax.broadcasted_iota(jnp.int32, (IRREPS, ROWS), 0) == irr).astype(F32)
    earlier = (
        lax.broadcasted_iota(jnp.int32, (ROWS, ROWS), 0) < lax.broadcasted_iota(jnp.int32, (ROWS, ROWS), 1)
    ).astype(F32)
    before = jnp.dot(onehot.astype(BF), earlier.astype(BF), preferred_element_type=F32)
    rank = jnp.sum(before * onehot, axis=0, keepdims=True)
    place = irr.astype(F32) * CAP + rank
    pos[0] = jnp.broadcast_to(place, (8, ROWS))

    def send_pos(k, c):
        pop(k).start()
        return c

    lax.fori_loop(1, NB, send_pos, 0)

    def pass_on(j):
        zop(j, "plus").wait_recv()
        zop(j, "far0").start()
        zop(j, "sib4").start()
        zop(j, "minus").wait_recv()
        zop(j, "far1").start()
        zop(j, "sib2").start()

    def own_chunk(j):
        zop(j, "plus").start()
        zop(j, "minus").start()

    def ring_pass(phase):
        for h in range(2):
            rop(h, phase, 0).wait_recv()
            rop(h, phase, 2).start()
            rop(h, phase, 1).wait_recv()
            rop(h, phase, 3).start()

    def ring_send(phase):
        for h in range(2):
            rop(h, phase, 0).start()
            rop(h, phase, 1).start()

    ring_pass(4)
    ring_send(3)
    ring_send(1)
    for h in range(2):
        rop(h, 4, 2).wait_recv()
        rop(h, 4, 3).wait_recv()
    ring_send(2)
    ring_pass(0)
    pass_on(0)
    own_chunk(2)
    ring_pass(3)
    ring_pass(1)
    pass_on(1)
    own_chunk(3)
    ring_pass(2)
    pass_on(2)
    for phase in (0, 3, 1, 2):
        for h in range(2):
            rop(h, phase, 2).wait_recv()
            rop(h, phase, 3).wait_recv()

    def wait_pos(k, c):
        pop(k).wait_recv()
        return c

    lax.fori_loop(1, NB, wait_pos, 0)

    def wload(j, n):
        src = w_ref if n == 0 else w_all.at[n]
        if j >= CHUNKS[-1][0]:
            there = held(j, n)
        else:
            there = wbuf.at[n, pl.ds(128 * (j % 2), PIECES[j])]
        return pltpu.make_async_copy(src.at[pl.ds(STARTS[j], PIECES[j])], there, wl.at[j, n])

    def loaded(c, n):
        return c < NC - 1 or n == 0

    def near(c):
        for j in CHUNKS[c]:
            zop(j, "sib0").wait_recv()
            zop(j, "sib2").wait_recv()
            zop(j, "sib4").wait_recv()
            for n in range(6):
                if loaded(c, n):
                    wload(j, n).start()

    def far(c):
        for j in CHUNKS[c]:
            zop(j, "far0").wait_recv()
            zop(j, "far1").wait_recv()
            zop(j, "sib6").start()
            if loaded(c, 6):
                wload(j, 6).start()

    def farther(c):
        for j in CHUNKS[c]:
            zop(j, "sib6").wait_recv()
            if loaded(c, 7):
                wload(j, 7).start()

    def aload(k):
        return pltpu.make_async_copy(a_all.at[k], abuf.at[k % ABUFS], al.at[k % ABUFS])

    def sort_block(k, c):
        hot = (
            lax.broadcasted_iota(jnp.int32, (SLOTS, ROWS), 0).astype(F32) == pos[k][0:1, :]
        ).astype(F32).astype(BF)
        pbuf[k] = hot
        aload(k).wait()
        for n in range(6):
            lanes = pl.ds(n * 512, 512)
            got = jnp.dot(hot, abuf[k % ABUFS, :, lanes], preferred_element_type=F32).astype(BF)
            xbuf[:, pl.ds(pl.multiple_of(k * CAP, CAP), CAP), lanes] = got.reshape(IRREPS, CAP, 512)

        @pl.when(k + ABUFS < NB)
        def _():
            aload(k + ABUFS).start()

        return c

    def multiply(c, first, last):
        last_chunk = c == NC - 1

        def irrep(n, carry):
            m = n // 2
            dz = m + m // 2 - 2 * (m // 3)
            which = 2 * ((z + dz) % 4) + (core + n % 2) % 2
            got = lax.dot_general(
                xbuf[which],
                wlast[n] if last_chunk else wbuf[n],
                (((1,), (1,)), ((), ())),
                preferred_element_type=F32,
            ).astype(BF)
            at = pl.ds(pl.multiple_of(which * CAP, CAP), CAP)
            if last_chunk:
                ylast[:, at, 0:NARROW] = got.reshape(NB, CAP, NARROW)
            else:
                ys[:, at, :] = got.reshape(NB, CAP, WIDE)
            return carry

        for j in CHUNKS[c]:
            for n in range(first, last):
                if loaded(c, n):
                    wload(j, n).wait()
        lax.fori_loop(first, last, irrep, 0)

    def give_back(c):
        last_chunk = c == NC - 1

        def back(u, carry):
            for v in range(4):
                k = 4 * u + v
                got = lax.dot_general(
                    ylast[k] if last_chunk else ys[k],
                    pbuf[k],
                    (((0,), (0,)), ((), ())),
                    preferred_element_type=F32,
                ).astype(BF)
                if last_chunk:
                    tlast[k] = got[0:NARROW]
                else:
                    tbuf[c, k] = got
            for v in range(4):
                if v == 0:

                    @pl.when(u > 0)
                    def _():
                        top(c, 4 * u).start()

                else:
                    top(c, 4 * u + v).start()
            return carry

        lax.fori_loop(0, NB // 4, back, 0)
        keep(c).start()

    pltpu.make_async_copy(amp_ref, abuf.at[0], al.at[0]).start()
    for k in range(1, ABUFS):
        aload(k).start()
    near(0)
    lax.fori_loop(0, NB, sort_block, 0)
    multiply(0, 0, 6)
    far(0)
    multiply(0, 6, 7)
    farther(0)
    multiply(0, 7, 8)
    give_back(0)
    pass_on(3)
    own_chunk(4)
    own_chunk(5)
    near(1)
    multiply(1, 0, 6)
    far(1)
    multiply(1, 6, 7)
    farther(1)
    multiply(1, 7, 8)
    give_back(1)
    pass_on(4)
    pass_on(5)
    near(2)
    multiply(2, 0, 4)
    far(2)
    multiply(2, 4, 7)
    farther(2)
    multiply(2, 7, 8)
    give_back(2)

    for c in range(NC):
        keep(c).wait()
        some = t_ref.at[pl.ds(0, (NB - 1) * width(c))]
        pltpu.make_async_copy(some, some, ts.at[c]).wait()
        pltpu.make_async_copy(some, some, tr.at[c]).wait()
    for j in range(NP):
        for name in ("plus", "minus", "far0", "far1", "sib0", "sib2", "sib4", "sib6"):
            zop(j, name).wait_send()
    for phase in range(5):
        for h in range(2):
            for n in range(4):
                rop(h, phase, n).wait_send()

    def done_pos(k, c):
        pop(k).wait_send()
        return c

    lax.fori_loop(1, NB, done_pos, 0)


def ladder(amplitudes, integrals, irreps):
    dma = pltpu.SemaphoreType.DMA
    hbm = pl.BlockSpec(memory_space=pl.ANY)
    t, _, _ = pl.pallas_call(
        ladder_kernel,
        out_shape=(
            pltpu.VMEM((SLAB, ROWS), BF),
            jax.ShapeDtypeStruct((NB, ROWS, KW), BF),
            jax.ShapeDtypeStruct((IRREPS, COLS, KW), BF),
        ),
        in_specs=[hbm, hbm, pl.BlockSpec(memory_space=pltpu.VMEM)],
        out_specs=(pl.BlockSpec(memory_space=pltpu.VMEM), hbm, hbm),
        scratch_shapes=[
            pltpu.VMEM((IRREPS, NB * CAP, KW), BF),
            pltpu.VMEM((IRREPS, WIDE, KW), BF),
            pltpu.VMEM((IRREPS, NARROW, KW), BF),
            pltpu.VMEM((ABUFS, ROWS, KW), BF),
            pltpu.VMEM((NB, SLOTS, ROWS), BF),
            pltpu.VMEM((NB, SLOTS, WIDE), BF),
            pltpu.VMEM((NB, SLOTS, 128), BF),
            pltpu.VMEM((NC - 1, NB, WIDE, ROWS), BF),
            pltpu.VMEM((NB, NARROW, ROWS), BF),
            pltpu.VMEM((NB, 8, ROWS), F32),
            dma((NP, 8)),
            dma((NP, 8)),
            dma((2, 5, 4)),
            dma((2, 5, 4)),
            dma((NB,)),
            dma((NB,)),
            dma((NC,)),
            dma((NC,)),
            dma((NC,)),
            dma((ABUFS,)),
            dma((NP, 8)),
        ],
        compiler_params=pltpu.CompilerParams(
            collective_id=0, has_side_effects=True, vmem_limit_bytes=57 * 1024 * 1024
        ),
        name="ladder",
    )(amplitudes, integrals, irreps)
    return t


GB = 1920
NG = SLAB // GB
NT = (((1,), (1,)), ((), ()))


def mirror_kernel(col_ref, t_ref, row_ref, out_ref, tf, even, odd):
    def widen(i, c):
        rows = pl.ds(pl.multiple_of(i * GB, GB), GB)
        tf[rows, :] = t_ref[rows, :].astype(F32)
        return c

    lax.fori_loop(0, NG, widen, 0)
    lane = lax.broadcasted_iota(jnp.int32, (ROWS, ROWS), 1)
    sub = lax.broadcasted_iota(jnp.int32, (ROWS, ROWS), 0)
    same = (lane == sub).astype(F32).astype(BF)
    swap = (sub == row_ref[...]).astype(F32).astype(BF)

    def pick(base, g):
        for q in range(GB // 8):
            some = [tf[pl.ds(col_ref[base + 8 * q + r], 1), :] for r in range(8)]
            g[8 * q : 8 * q + 8, :] = jnp.concatenate(some, axis=0)

    def add(base, g):
        here = lax.dot_general(same, t_ref[pl.ds(base, GB), :], NT, preferred_element_type=F32)
        there = lax.dot_general(swap, g[...].astype(BF), NT, preferred_element_type=F32)
        out_ref[:, pl.ds(base, GB)] = (here + there).astype(BF)

    pick(0, even)

    def two(i, c):
        first = pl.multiple_of(2 * i * GB, GB)
        second = pl.multiple_of(first + GB, GB)
        third = pl.multiple_of(first + 2 * GB, GB)
        pick(second, odd)
        add(first, even)
        pick(third, even)
        add(second, odd)
        return c

    lax.fori_loop(0, NG // 2, two, 0)
    add((NG - 1) * GB, even)


def mirror(t, row_mirror, col_mirror):
    vmem = pl.BlockSpec(memory_space=pltpu.VMEM)
    return pl.pallas_call(
        mirror_kernel,
        out_shape=jax.ShapeDtypeStruct((ROWS, SLAB), BF),
        in_specs=[pl.BlockSpec(memory_space=pltpu.SMEM), vmem, vmem],
        out_specs=vmem,
        scratch_shapes=[
            pltpu.VMEM((SLAB, ROWS), F32),
            pltpu.VMEM((GB, ROWS), F32),
            pltpu.VMEM((GB, ROWS), F32),
        ],
        compiler_params=pltpu.CompilerParams(vmem_limit_bytes=32 * 1024 * 1024),
        name="mirror",
    )(col_mirror, t, row_mirror)


def body(amplitudes, integrals, irreps, row_mirror, col_mirror):
    w = jnp.swapaxes(integrals[0], 0, 1)
    t = ladder(amplitudes, w, irreps.reshape(1, ROWS))
    return mirror(t, row_mirror.reshape(1, ROWS), col_mirror)


def solution(mesh):
    return jax.shard_map(
        body,
        mesh=mesh,
        in_specs=(
            P(("row", "col"), None),
            P("col", None, "row"),
            P(("row", "col")),
            P(("row", "col")),
            P(),
        ),
        out_specs=P(("row", "col"), None),
        check_vma=False,
    )
```
